256 devices in a mesh: row: 8 (over y, core), col: 32 (over z, x).
Axes of the slice: x: 4, y: 4, z: 8, core: 2. Of those that a mesh axis runs over, the one named last changes fastest.
Arguments:
- right_side: bfloat16 [8, 32, 256, 512], P(None, 'col'), may hold values from -6 to 6
- inverses: bfloat16 [8, 32, 256, 256], P(None, 'col'), may hold values from -0.375 to 0.375
- factor_blocks: bfloat16 [224, 32, 2, 256, 256], P('row', 'col'), may hold values from -0.03125 to 0.03125
- pattern: int32 [224, 32, 2], P('row', 'col'), may hold values from 0 to 3, as said below
Outputs:
- solution: bfloat16 [8, 32, 256, 512], P(None, 'col')
The draws below stay inside these ranges and needn't reach their ends.
Inputs may be any that keep to these rules, and one draw needn't show every extreme that they name: The 2 entries of one slot list of pattern name different solved blocks.
All inputs are finite; a program needn't handle non-finite values.
Results may differ from the reference program's by a relative error of at most 0.022.
Values may be sent and summed in bfloat16 or wider, within the bound.
No kernel may reach another device: no remote copies, remote signals or barrier semaphores. Data moves between devices by JAX's collectives and lax.ppermute only.
A program may use at most 128 MiB of HBM per device.

```python
import jax
import jax.numpy as jnp
from jax import lax

BS = 256
NRHS = 512
LEVELS = 8
K = 2
TPC = 1
PAIRS = 28
BLOCKS = 32
SOURCES = 4
FACTOR_ROWS = 224
N_ROW = 8


def draw_pattern(key, part):
    first_key = jax.random.fold_in(key, 11)
    second_key = jax.random.fold_in(key, 12)
    shape = (FACTOR_ROWS, BLOCKS)
    first = jax.random.randint(first_key, shape, 0, SOURCES)
    step_size = jax.random.randint(second_key, shape, 1, SOURCES)
    second = (first + step_size) % SOURCES
    return jnp.stack([first, second], axis=-1).astype(jnp.int32)


def block_scale(rng, extent, cuts, low, high):
    factor_of = 1.0
    for axis_at, shards_of in cuts:
        draws = jax.random.uniform(jax.random.fold_in(jax.random.fold_in(rng, 6), axis_at), (shards_of,), jnp.float32, low / len(cuts), high / len(cuts))
        factor_of = factor_of * jnp.repeat(jnp.exp(draws), extent[axis_at] // shards_of).reshape((-1,) + (1,) * (len(extent) - 1 - axis_at))
    return factor_of


def gaussian(own_key, extent, spread, bound, pieces=(), kind=jnp.bfloat16):
    entries = spread * jax.random.normal(own_key, extent, jnp.float32)
    if pieces:
        entries = entries * block_scale(own_key, extent, pieces, -0.22, 0.18)
    return jnp.clip(entries, -bound, bound).astype(kind)


def setup_inputs(seed: int = 0) -> dict:
    key_list = jax.random.split(jax.random.key(seed), 5)
    return {
        "right_side": gaussian(key_list[0], (LEVELS, BLOCKS, BS, NRHS), 1.0, 6.0, ((1, 32),)),
        "inverses": gaussian(key_list[1], (LEVELS, BLOCKS, BS, BS), BS ** -0.5, 0.375, ((1, 32),)),
        "factor_blocks": gaussian(key_list[2], (FACTOR_ROWS, BLOCKS, K, BS, BS), (BS * K * N_ROW * LEVELS) ** -0.5, 0.03125, ((0, 8), (1, 32))),
        "pattern": draw_pattern(jax.random.fold_in(key_list[4], 71), 0),
    }


def reference(right_side, inverses, factor_blocks, pattern):
    factor_view = factor_blocks.reshape(N_ROW, PAIRS, BLOCKS, K, BS, BS)
    pattern_view = pattern.reshape(N_ROW, PAIRS, BLOCKS, K)
    row_ids = jnp.arange(N_ROW, dtype=jnp.int32)[:, None, None]
    solutions = []
    for current in range(LEVELS):
        totals = right_side[current].astype(jnp.float32)
        if current > 0:
            partial_value = jnp.zeros((N_ROW, BLOCKS, BS, NRHS), jnp.float32)
            for earlier in range(current):
                pair_index = current * (current - 1) // 2 + earlier
                picked = pattern_view[:, pair_index]
                column = ((row_ids + N_ROW * (picked // TPC)) * TPC + picked % TPC).astype(jnp.int32)
                sources = solutions[earlier][column]
                partial_value = partial_value + jnp.einsum("rjkab,rjkbn->rjan", factor_view[:, pair_index].astype(jnp.float32), sources.astype(jnp.float32))
            rounded = lax.optimization_barrier(partial_value.astype(jnp.bfloat16)).astype(jnp.float32)
            totals = totals - jnp.sum(rounded, axis=0)
        scaled = lax.optimization_barrier(totals.astype(jnp.bfloat16)).astype(jnp.float32)
        solved = jnp.einsum("jab,jbn->jan", inverses[current].astype(jnp.float32), scaled).astype(jnp.bfloat16)
        solutions.append(solved)
    return jnp.stack(solutions)
```

```python
import functools

import jax
import jax.numpy as jnp
from jax import lax
from jax.experimental import pallas as pl
from jax.experimental.pallas import tpu as pltpu
from jax.sharding import PartitionSpec as P

LEVELS = 8
PAIRS = 28
BS = 256
NRHS = 512
PIECE = 64
PART = 2 * PIECE
AXES = ("row", "col")
CHUNKS = ((0, 3), (3, 10), (10, 21), (21, 28))
NT = (((1,), (1,)), ((), ()))
BF = jnp.bfloat16
F32 = jnp.float32
TASK = 2 * PAIRS
AT_Y, AT_H, AT_Z, AT_X = (4 * TASK + n for n in range(4))
TEAMS = [[4 * z + x, 4 * z + 4 + x] for z in (0, 2, 4, 6) for x in range(4)]


def moves(to):
    pairs = []
    for y in range(4):
        for h in range(2):
            for z in range(8):
                for x in range(4):
                    ty, th, tz, tx = to(y, h, z, x)
                    pairs.append(((y * 2 + h) * 32 + z * 4 + x, (ty * 2 + th) * 32 + tz * 4 + tx))
    return pairs


def exchange(y, h, z, x):
    return 2 * (z % 2) + y % 2, h, 2 * (z // 2) + y // 2, x


def level_z(s):
    return lambda y, h, z, x: (y, h, (z + 2 * s) % 8, x)


def cross(t):
    return lambda y, h, z, x: (y // 2 * 2 + x // 2, h, z, (y % 2 * 2 + x % 2) ^ t)


SWAP = moves(lambda y, h, z, x: (y, 1 - h, z, x))
NEIGHBOUR = moves(lambda y, h, z, x: (y, h, z ^ 1, x))
EXCHANGE = moves(exchange)
LEVEL_Z = [moves(level_z(s)) for s in range(4)]
FIRST_Z = [moves(lambda *at, s=s: level_z(s)(*exchange(*at))) for s in range(4)]
CROSS = [moves(cross(t)) for t in range(4)]
ALONG_Y = [moves(lambda y, h, z, x, s=s: ((y + s) % 4, h, z, x)) for s in range(4)]
COLLECT = [
    moves(lambda y, h, z, x, s=s: ((2 * (z % 2) + y % 2 + s) % 4, h, 2 * (z // 2) + y // 2, x)) for s in range(4)
]


def dot_nt(a, b):
    return lax.dot_general(a, b, NT, preferred_element_type=F32)


def pair_of(level, earlier):
    return level * (level - 1) // 2 + earlier


def chunk_of(pair):
    return next((n, pair - a) for n, (a, b) in enumerate(CHUNKS) if a <= pair < b)


def factor_spec(pair, side):
    at = chunk_of(pair)[1]
    return pl.BlockSpec((1, 1, 1, 2, BS, BS), lambda i, meta: ((meta[AT_Z] + side) % 2, at, 0, 0, 0, 0))


def factor_of(pair, side, factors):
    return factors[side // 2][chunk_of(pair)[0]]


def whole(shape):
    return pl.BlockSpec(shape, lambda i, meta: (0,) * len(shape))


def call(body, name, grid, specs, out_specs, out_shape, scratch, mib, flops, size, alias=None):
    return pl.pallas_call(
        body,
        name=name,
        grid_spec=pltpu.PrefetchScalarGridSpec(
            num_scalar_prefetch=1,
            grid=grid,
            in_specs=specs,
            out_specs=out_specs,
            scratch_shapes=scratch,
        ),
        out_shape=out_shape,
        compiler_params=pltpu.CompilerParams(vmem_limit_bytes=mib << 20),
        cost_estimate=pl.CostEstimate(flops=flops, bytes_accessed=size, transcendentals=0),
        input_output_aliases=alias or {},
    )


def task_term(meta, pair, side, sources, blocks):
    at = side * TASK + 2 * pair
    return dot_nt(sources[meta[at]], blocks[0, 0, 0, 0]) + dot_nt(sources[meta[at + 1]], blocks[0, 0, 0, 1])


def earlier_terms(level, meta, sources, factors):
    count = level - 1
    specs, operands = [], []
    for m in range(count):
        pair = pair_of(level, m)
        specs.append(whole((8, PART, BS)))
        operands.append(sources[m])
        for side in range(4):
            specs.append(factor_spec(pair, side))
            operands.append(factor_of(pair, side, factors))

    def body(meta, *refs):
        ins, out = refs[:-1], refs[-1]
        for row in range(2):
            total = None
            for m in range(count):
                for side in (row, row + 2):
                    term = task_term(meta, pair_of(level, m), side, ins[5 * m], ins[5 * m + 1 + side])
                    total = term if total is None else total + term
            out[row] = total

    return call(
        body, f"earlier_{level}", (1,), specs, whole((2, PART, BS)),
        jax.ShapeDtypeStruct((2, PART, BS), F32), [], 48,
        count * 8 * BS**3, count * (3 << 19),
    )(meta, *operands)


def last_term(level, meta, arrived, before, factors):
    pair = pair_of(level, level - 1)
    specs = [whole((4, PIECE, BS))] * 4 + [factor_spec(pair, side) for side in range(4)]
    operands = [*arrived] + [factor_of(pair, side, factors) for side in range(4)]
    if before is not None:
        specs.append(whole((2, PART, BS)))
        operands.append(before)

    def body(meta, *refs):
        ins, outs, total = refs[: len(operands)], refs[len(operands) : -1], refs[-1]
        sources = outs[0]
        for t in range(4):
            at = t // 2 * PIECE
            sources[t % 2 * 4 : t % 2 * 4 + 4, at : at + PIECE, :] = ins[t][...]
        for row in range(2):
            value = None if before is None else ins[8][row]
            for side in (row, row + 2):
                term = task_term(meta, pair, side, sources, ins[4 + side])
                value = term if value is None else value + term
            total[row] = value
        y, z, x = meta[AT_Y], meta[AT_Z], meta[AT_X]
        for s in range(4):
            to = (y + s) % 4
            rows = pl.multiple_of((to + x // 2) % 2 * PIECE, PIECE)
            outs[1 + s][...] = total[(to // 2 + z) % 2, pl.ds(rows, PIECE), :].astype(BF)

    out = call(
        body, f"last_{level}", (1,), specs, [whole((8, PART, BS))] + [whole((PIECE, BS))] * 4,
        [jax.ShapeDtypeStruct((8, PART, BS), BF)] + [jax.ShapeDtypeStruct((PIECE, BS), BF)] * 4,
        [pltpu.VMEM((2, PART, BS), F32)], 24, 8 * BS**3, 3 << 20,
    )(meta, *operands)
    return out[0], out[1:]


def columns_of(meta, right):
    first = meta[AT_H] * BS + meta[AT_Y] * PIECE
    rows = lax.broadcasted_iota(jnp.int32, (PIECE, NRHS), 0)
    columns = lax.broadcasted_iota(jnp.int32, (PIECE, NRHS), 1)
    return dot_nt((columns == rows + first).astype(F32).astype(BF), right).astype(BF)


def solve_first(meta, right_side, inverses):
    def body(meta, right, inverse, out):
        out[...] = dot_nt(columns_of(meta, right[0, 0]), inverse[0, 0]).astype(BF)

    return call(
        body, "solve_0", (1,), [whole((1, 1, BS, NRHS)), whole((1, 1, BS, BS))], whole((PIECE, BS)),
        jax.ShapeDtypeStruct((PIECE, BS), BF), [], 16, 3 * PIECE * BS * NRHS, 1 << 19,
    )(meta, right_side, inverses)


def right_pieces(meta, right_side):
    def body(meta, right, out):
        out[0] = columns_of(meta, right[0, 0])

    return call(
        body, "right_pieces", (LEVELS,), [pl.BlockSpec((1, 1, BS, NRHS), lambda i, meta: (i, 0, 0, 0))],
        pl.BlockSpec((1, PIECE, BS), lambda i, meta: (i, 0, 0)),
        jax.ShapeDtypeStruct((LEVELS, PIECE, BS), BF), [], 16, LEVELS * 2 * PIECE * BS * NRHS, 5 << 19,
    )(meta, right_side)


def solve(level, meta, pieces, right, inverses):
    def body(meta, *refs):
        parts, (right, inverse, out) = refs[:-3], refs[-3:]
        summed = parts[0][...].astype(F32)
        for part in parts[1:]:
            summed = summed + part[...].astype(F32)
        totals = right[0].astype(F32) - summed
        out[...] = dot_nt(totals.astype(BF), inverse[...].reshape(BS, BS)).astype(BF)

    specs = [whole((PIECE, BS))] * len(pieces) + [
        pl.BlockSpec((1, PIECE, BS), lambda i, meta: (level, 0, 0)),
        pl.BlockSpec((1, 1, 1, BS, BS), lambda i, meta: (meta[AT_Y] // 2, level, 0, 0, 0))
        if level > 1
        else whole((1, 1, BS, BS)),
    ]
    return call(
        body, f"solve_{level}", (1,), specs, whole((PIECE, BS)),
        jax.ShapeDtypeStruct((PIECE, BS), BF), [], 16, 2 * PIECE * BS * BS, 1 << 18,
    )(meta, *pieces, right, inverses)


def turned(stacked):
    rows = lax.broadcasted_iota(jnp.int32, (BS, BS), 0)
    columns = lax.broadcasted_iota(jnp.int32, (BS, BS), 1)
    return dot_nt((rows == columns).astype(F32).astype(BF), stacked).astype(BF)


def first_outputs(meta, gathered):
    count = gathered.shape[1]

    def body(meta, pieces, out, stacked):
        for r in range(8):
            at = (r % 2) * BS + (r // 2) * PIECE
            stacked[at : at + PIECE, :] = pieces[r, 0]
        out[0, 0] = turned(stacked[...])

    return call(
        body, "first_outputs", (count,),
        [pl.BlockSpec((8, 1, PIECE, BS), lambda i, meta: (0, i, 0, 0))],
        pl.BlockSpec((1, 1, BS, NRHS), lambda i, meta: (i, 0, 0, 0)),
        jax.ShapeDtypeStruct((LEVELS, 1, BS, NRHS), BF),
        [pltpu.VMEM((NRHS, BS), BF)], 16, count * 2 * BS * BS * NRHS, count << 19,
    )(meta, gathered)


def last_outputs(meta, mine, others, out):
    count = mine.shape[1]
    start = LEVELS - count

    def body(meta, mine, others, _, out, stacked):
        y, h = meta[AT_Y], meta[AT_H]
        for side, half in ((mine, h), (others, 1 - h)):
            for s in range(4):
                at = pl.multiple_of(half * BS + ((y - s + 4) % 4) * PIECE, PIECE)
                stacked[pl.ds(at, PIECE), :] = side[s, 0]
        out[0, 0] = turned(stacked[...])

    return call(
        body, "last_outputs", (count,),
        [pl.BlockSpec((4, 1, PIECE, BS), lambda i, meta: (0, i, 0, 0))] * 2
        + [pl.BlockSpec(memory_space=pl.ANY)],
        pl.BlockSpec((1, 1, BS, NRHS), lambda i, meta: (start + i, 0, 0, 0)),
        jax.ShapeDtypeStruct((LEVELS, 1, BS, NRHS), BF),
        [pltpu.VMEM((NRHS, BS), BF)], 16, count * 2 * BS * BS * NRHS, count << 19,
        alias={3: 0},
    )(meta, mine, others, out)


def after(value, event):
    return lax.optimization_barrier((value, event))[0]


def shards(right_side, inverses, factor_blocks, pattern):
    row, col = lax.axis_index("row"), lax.axis_index("col")
    y, h, z, x = row // 2, row % 2, col // 4, col % 4
    move = functools.partial(lax.ppermute, axis_name=AXES)

    places = jnp.stack([y, h, z % 2, x]).astype(jnp.int32)
    start = jnp.concatenate([jnp.zeros((4 * TASK,), jnp.int32), places])
    solved = solve_first(start, right_side, inverses)
    solutions = [solved]

    picked = pattern.reshape(1, TASK)
    picked = jnp.concatenate([picked, move(picked, perm=SWAP)])
    picked = jnp.stack([picked, move(picked, perm=NEIGHBOUR)], axis=1)
    group = (jnp.stack([h, 1 - h]) + x) % 2
    place = 4 * group[:, None, None] + (z // 2 - picked + 8) % 4
    meta = jnp.concatenate([place.reshape(4 * TASK).astype(jnp.int32), places])

    mine, theirs = [None] * 4, [None] * 4
    factors = [mine, theirs]

    def both(value):
        return lax.all_gather(value, "col", axis_index_groups=TEAMS)

    def fetch(n, event):
        mine[n] = both(after(factor_blocks[CHUNKS[n][0] : CHUNKS[n][1]], event))

    def share(n, event):
        theirs[n] = move(after(mine[n], event), perm=SWAP)

    fetch(0, start)
    share(0, solved)
    local = both(inverses)
    fetch(1, solved)

    sources = []
    for level in range(1, LEVELS):
        if level == 1:
            block = jnp.stack([move(solved, perm=way) for way in FIRST_Z])
            right = move(after(right_pieces(start, right_side), block), perm=EXCHANGE)
            first = move(after(inverses[1:2], block), perm=EXCHANGE)
            fetch(2, block)
        else:
            block = jnp.stack([solved] + [move(solved, perm=way) for way in LEVEL_Z[1:]])
        arrived = [move(block, perm=way) for way in CROSS]
        before = earlier_terms(level, meta, sources, factors) if level > 1 else None
        stacked, parts = last_term(level, meta, arrived, before, factors)
        sources.append(stacked)
        pieces = [parts[0]] + [move(parts[s], perm=ALONG_Y[s]) for s in (1, 2, 3)]
        solved = solve(level, meta, pieces, right, local if level > 1 else first)
        solutions.append(solved)
        if level == 1:
            fetch(3, solved)
        if level in (2, 4, 6):
            share(level // 2, solved)

    body = jnp.concatenate([solutions[0][None], move(jnp.stack(solutions[1:6]), perm=EXCHANGE)])
    out = first_outputs(meta, lax.all_gather(body, "row"))
    tail = jnp.stack(solutions[6:])
    mine = jnp.stack([move(tail, perm=way) for way in COLLECT])
    return last_outputs(meta, mine, move(mine, perm=SWAP), out)


def solution(mesh):
    in_specs = (
        P(None, "col", None, None),
        P(None, "col", None, None),
        P("row", "col", None, None, None),
        P("row", "col", None),
    )
    out_specs = P(None, "col", None, None)
    return jax.shard_map(shards, mesh=mesh, in_specs=in_specs, out_specs=out_specs, check_vma=False)
```

```python
import functools

import jax
import jax.numpy as jnp
from jax import lax
from jax.experimental import pallas as pl
from jax.experimental.pallas import tpu as pltpu
from jax.sharding import PartitionSpec as P

LEVELS = 8
PAIRS = 28
BS = 256
NRHS = 512
PIECE = 64
PART = 2 * PIECE
AXES = ("row", "col")
CHUNKS = ((0, 1), (1, 3), (3, 10), (10, 21), (21, 28))
PERMUTED = 2
SHARED = ((0,), (1,), (2,), (3,), (), (4,))
NT = (((1,), (1,)), ((), ()))
BF = jnp.bfloat16
F32 = jnp.float32
TASK = 2 * PAIRS
AT_Y, AT_H, AT_Z, AT_X = (4 * TASK + n for n in range(4))
TEAMS = [[4 * z + x, 4 * z + 4 + x] for z in (0, 2, 4, 6) for x in range(4)]

def moves(to):
    pairs = []
    for y in range(4):
        for h in range(2):
            for z in range(8):
                for x in range(4):
                    ty, th, tz, tx = to(y, h, z, x)
                    pairs.append(((y * 2 + h) * 32 + z * 4 + x, (ty * 2 + th) * 32 + tz * 4 + tx))
    return pairs


def exchange(y, h, z, x):
    return 2 * (z % 2) + y % 2, h, 2 * (z // 2) + y // 2, x


def level_z(s):
    return lambda y, h, z, x: (y, h, (z + 2 * s) % 8, x)


def cross(t):
    return lambda y, h, z, x: (y // 2 * 2 + x // 2, h, z, (y % 2 * 2 + x % 2) ^ t)


SWAP = moves(lambda y, h, z, x: (y, 1 - h, z, x))
NEIGHBOUR = moves(lambda y, h, z, x: (y, h, z ^ 1, x))
EXCHANGE = moves(exchange)
LEVEL_Z = [moves(level_z(s)) for s in range(4)]
FIRST_Z = [moves(lambda *at, s=s: level_z(s)(*exchange(*at))) for s in range(4)]
CROSS = [moves(cross(t)) for t in range(4)]
INVERSES = [
    ((y * 2 + h) * 32 + z * 4 + x, (y * 2 + h) * 32 + (z ^ 1) * 4 + x)
    for y in range(4)
    for h in range(2)
    for z in range(8)
    for x in range(4)
    if y // 2 == z % 2
]
INVERSE_CHUNKS = ((1, 2), (2, 4), (4, 8))
ALONG_Y = [moves(lambda y, h, z, x, s=s: ((y + s) % 4, h, z, x)) for s in range(4)]
COLLECT = [
    moves(lambda y, h, z, x, s=s: ((2 * (z % 2) + y % 2 + s) % 4, h, 2 * (z // 2) + y // 2, x)) for s in range(4)
]


def dot_nt(a, b):
    return lax.dot_general(a, b, NT, preferred_element_type=F32)


def pair_of(level, earlier):
    return level * (level - 1) // 2 + earlier


def chunk_of(pair):
    return next((n, pair - a) for n, (a, b) in enumerate(CHUNKS) if a <= pair < b)


def factor_spec(pair, side):
    chunk, at = chunk_of(pair)
    if side % 2 == 0:
        return pl.BlockSpec((1, 1, 2, BS, BS), lambda i, meta: (pair, 0, 0, 0, 0))
    if chunk < PERMUTED:
        return pl.BlockSpec((1, 1, 2, BS, BS), lambda i, meta: (at, 0, 0, 0, 0))
    return pl.BlockSpec((1, 1, 1, 2, BS, BS), lambda i, meta: (1 - meta[AT_Z], at, 0, 0, 0, 0))


def factor_of(pair, side, factors):
    if side % 2 == 0:
        return in_hbm(factors[side])
    chunk = chunk_of(pair)[0]
    return factors[side][chunk] if chunk < PERMUTED else in_hbm(factors[side][chunk])


def in_hbm(value):
    return pltpu.with_memory_space_constraint(value, pltpu.HBM)


def whole(shape):
    return pl.BlockSpec(shape, lambda i, meta: (0,) * len(shape))


def call(body, name, grid, specs, out_specs, out_shape, scratch, mib, flops, size, alias=None):
    return pl.pallas_call(
        body,
        name=name,
        grid_spec=pltpu.PrefetchScalarGridSpec(
            num_scalar_prefetch=1,
            grid=grid,
            in_specs=specs,
            out_specs=out_specs,
            scratch_shapes=scratch,
        ),
        out_shape=out_shape,
        compiler_params=pltpu.CompilerParams(vmem_limit_bytes=mib << 20),
        cost_estimate=pl.CostEstimate(flops=flops, bytes_accessed=size, transcendentals=0),
        input_output_aliases=alias or {},
    )


def task_term(meta, pair, side, sources, blocks):
    at = side * TASK + 2 * pair
    lead = (0,) * (len(blocks.shape) - 3)
    return dot_nt(sources[meta[at]], blocks[(*lead, 0)]) + dot_nt(sources[meta[at + 1]], blocks[(*lead, 1)])


def earlier_terms(level, meta, sources, factors):
    count = level - 1
    specs, operands = [], []
    for m in range(count):
        pair = pair_of(level, m)
        specs.append(whole((8, PART, BS)))
        operands.append(in_hbm(sources[m]))
        for side in range(4):
            specs.append(factor_spec(pair, side))
            operands.append(factor_of(pair, side, factors))

    def body(meta, *refs):
        ins, out = refs[:-1], refs[-1]
        for row in range(2):
            total = None
            for m in range(count):
                for side in (row, row + 2):
                    term = task_term(meta, pair_of(level, m), side, ins[5 * m], ins[5 * m + 1 + side])
                    total = term if total is None else total + term
            out[row] = total

    return call(
        body, f"earlier_{level}", (1,), specs, whole((2, PART, BS)),
        jax.ShapeDtypeStruct((2, PART, BS), F32), [], 4 + 4 * count,
        count * 8 * BS**3, count * (3 << 19),
    )(meta, *operands)


def last_term(level, meta, arrived, before, factors):
    pair = pair_of(level, level - 1)
    specs = [whole((4, PIECE, BS))] * 4 + [factor_spec(pair, side) for side in range(4)]
    operands = [*arrived] + [factor_of(pair, side, factors) for side in range(4)]
    if before is not None:
        specs.append(whole((2, PART, BS)))
        operands.append(before)

    def body(meta, *refs):
        ins, outs, total = refs[: len(operands)], refs[len(operands) : -1], refs[-1]
        sources = outs[0]
        for t in range(4):
            at = t // 2 * PIECE
            sources[t % 2 * 4 : t % 2 * 4 + 4, at : at + PIECE, :] = ins[t][...]
        for row in range(2):
            value = None if before is None else ins[8][row]
            for side in (row, row + 2):
                term = task_term(meta, pair, side, sources, ins[4 + side])
                value = term if value is None else value + term
            total[row] = value
        y, z, x = meta[AT_Y], meta[AT_Z], meta[AT_X]
        for s in range(4):
            to = (y + s) % 4
            rows = pl.multiple_of((to + x // 2) % 2 * PIECE, PIECE)
            outs[1 + s][...] = total[(to // 2 + z) % 2, pl.ds(rows, PIECE), :].astype(BF)

    out = call(
        body, f"last_{level}", (1,), specs, [whole((8, PART, BS))] + [whole((PIECE, BS))] * 4,
        [pltpu.HBM((8, PART, BS), BF)] + [jax.ShapeDtypeStruct((PIECE, BS), BF)] * 4,
        [pltpu.VMEM((2, PART, BS), F32)], 10, 8 * BS**3, 3 << 20,
    )(meta, *operands)
    return out[0], out[1:]


def columns_of(meta, right):
    first = meta[AT_H] * BS + meta[AT_Y] * PIECE
    rows = lax.broadcasted_iota(jnp.int32, (PIECE, NRHS), 0)
    columns = lax.broadcasted_iota(jnp.int32, (PIECE, NRHS), 1)
    return dot_nt((columns == rows + first).astype(F32).astype(BF), right).astype(BF)


def solve_first(meta, right_side, inverses):
    def body(meta, right, inverse, out):
        out[...] = dot_nt(columns_of(meta, right[0, 0]), inverse[0, 0]).astype(BF)

    return call(
        body, "solve_0", (1,), [whole((1, 1, BS, NRHS)), whole((1, 1, BS, BS))], whole((PIECE, BS)),
        jax.ShapeDtypeStruct((PIECE, BS), BF), [], 16, 3 * PIECE * BS * NRHS, 1 << 19,
    )(meta, right_side, inverses)


def right_pieces(meta, right_side):
    def body(meta, right, out):
        out[0] = columns_of(meta, right[0, 0])

    return call(
        body, "right_pieces", (LEVELS,), [pl.BlockSpec((1, 1, BS, NRHS), lambda i, meta: (i, 0, 0, 0))],
        pl.BlockSpec((1, PIECE, BS), lambda i, meta: (i, 0, 0)),
        jax.ShapeDtypeStruct((LEVELS, PIECE, BS), BF), [], 16, LEVELS * 2 * PIECE * BS * NRHS, 5 << 19,
    )(meta, right_side)


def solve(level, meta, pieces, right, inverses, passed):
    n, first = next((n, a) for n, (a, b) in enumerate(INVERSE_CHUNKS) if a <= level < b)

    def body(meta, *refs):
        parts, (right, own, near, out) = refs[:-4], refs[-4:]
        summed = parts[0][...].astype(F32)
        for part in parts[1:]:
            summed = summed + part[...].astype(F32)
        scaled = (right[0].astype(F32) - summed).astype(BF)
        here = meta[AT_Y] // 2 == meta[AT_Z]

        @pl.when(here)
        def _():
            out[...] = dot_nt(scaled, own[0, 0]).astype(BF)

        @pl.when(jnp.logical_not(here))
        def _():
            out[...] = dot_nt(scaled, near[0, 0]).astype(BF)

    specs = [whole((PIECE, BS))] * len(pieces) + [
        pl.BlockSpec((1, PIECE, BS), lambda i, meta: (level, 0, 0)),
        pl.BlockSpec((1, 1, BS, BS), lambda i, meta: (level, 0, 0, 0)),
        pl.BlockSpec((1, 1, BS, BS), lambda i, meta: (level - first, 0, 0, 0)),
    ]
    return call(
        body, f"solve_{level}", (1,), specs, whole((PIECE, BS)),
        jax.ShapeDtypeStruct((PIECE, BS), BF), [], 6, 2 * PIECE * BS * BS, 1 << 18,
    )(meta, *pieces, right, inverses, passed[n])


def turned(stacked):
    rows = lax.broadcasted_iota(jnp.int32, (BS, BS), 0)
    columns = lax.broadcasted_iota(jnp.int32, (BS, BS), 1)
    return dot_nt((rows == columns).astype(F32).astype(BF), stacked).astype(BF)


def outputs(meta, start, mine, others, out=None):
    count = mine.shape[1]

    def body(meta, mine, others, *refs):
        out, stacked = refs[-2:]
        y, h = meta[AT_Y], meta[AT_H]
        for side, half in ((mine, h), (others, 1 - h)):
            for s in range(4):
                at = pl.multiple_of(half * BS + ((y - s + 4) % 4) * PIECE, PIECE)
                stacked[pl.ds(at, PIECE), :] = side[s, 0]
        out[0, 0] = turned(stacked[...])

    return call(
        body, f"outputs_{start}", (count,),
        [pl.BlockSpec((4, 1, PIECE, BS), lambda i, meta: (0, i, 0, 0))] * 2
        + [pl.BlockSpec(memory_space=pl.ANY)] * (out is not None),
        pl.BlockSpec((1, 1, BS, NRHS), lambda i, meta: (start + i, 0, 0, 0)),
        jax.ShapeDtypeStruct((LEVELS, 1, BS, NRHS), BF),
        [pltpu.VMEM((NRHS, BS), BF)], 6, count * 2 * BS * BS * NRHS, count << 19,
        alias=None if out is None else {3: 0},
    )(meta, mine, others, *(() if out is None else (out,)))


def joined(pieces):
    return jnp.concatenate(pieces).reshape(len(pieces), *pieces[0].shape)


def after(value, event):
    return lax.optimization_barrier((value, event))[0]


def shards(right_side, inverses, factor_blocks, pattern):
    row, col = lax.axis_index("row"), lax.axis_index("col")
    y, h, z, x = row // 2, row % 2, col // 4, col % 4
    move = functools.partial(lax.ppermute, axis_name=AXES)

    places = jnp.stack([y, h, z % 2, x]).astype(jnp.int32)
    start = jnp.concatenate([jnp.zeros((4 * TASK,), jnp.int32), places])
    solved = solve_first(start, right_side, inverses)

    picked = pattern.reshape(1, TASK)
    picked = jnp.concatenate([picked, move(picked, perm=SWAP)])
    picked = jnp.stack([picked, move(picked, perm=NEIGHBOUR)], axis=1)
    group = (jnp.stack([h, 1 - h]) + x) % 2
    place = 4 * group[:, None, None] + (z // 2 - picked + 8) % 4
    meta = jnp.concatenate([place.reshape(4 * TASK).astype(jnp.int32), places])

    core = move(factor_blocks, perm=SWAP)
    near, far = [None] * len(CHUNKS), [None] * len(CHUNKS)
    factors = [factor_blocks, near, core, far]

    def both(value):
        return lax.all_gather(value, "col", axis_index_groups=TEAMS)

    def fetch(n, event):
        part = after(factor_blocks[CHUNKS[n][0] : CHUNKS[n][1]], event)
        near[n] = move(part, perm=NEIGHBOUR) if n < PERMUTED else both(part)

    def share(n, event):
        far[n] = move(after(near[n], event), perm=SWAP)

    fetch(0, start)
    fetch(2, start)
    fetch(3, start)
    first = move(inverses[1:2], perm=INVERSES)
    solved, meta, near[0], first = lax.optimization_barrier((solved, meta, near[0], first))
    passed = [first]

    sources = []
    for level in range(1, LEVELS):
        if level == 1:
            held = [move(solved, perm=way) for way in FIRST_Z]
            solutions = held[:1]
            block = joined(held)
            right = move(after(right_pieces(start, right_side), block), perm=EXCHANGE)
        else:
            block = joined([solved] + [move(solved, perm=way) for way in LEVEL_Z[1:]])
        arrived = [move(block, perm=way) for way in CROSS]
        if level < PERMUTED:
            fetch(level, block)
        if level <= len(SHARED):
            for n in SHARED[level - 1]:
                share(n, block)
        if level == 2:
            fetch(4, block)
        if level < len(INVERSE_CHUNKS):
            a, b = INVERSE_CHUNKS[level]
            passed.append(move(after(inverses[a:b], block), perm=INVERSES))
        if level == 6:
            early = [move(after(joined(solutions[:5]), block), perm=way) for way in COLLECT]
        if level == 7:
            mine = joined(early)
            out = outputs(meta, 0, mine, move(after(mine, block), perm=SWAP))
        before = earlier_terms(level, meta, sources, factors) if level > 1 else None
        stacked, parts = last_term(level, meta, arrived, before, factors)
        sources.append(stacked)
        pieces = [parts[0]] + [move(parts[s], perm=ALONG_Y[s]) for s in (1, 2, 3)]
        if level == LEVELS - 1:
            pieces, out = lax.optimization_barrier((pieces, out))
        solved = solve(level, meta, pieces, right, inverses, passed)
        solutions.append(solved)

    tail = joined(solutions[5:])
    mine = joined([move(tail, perm=way) for way in COLLECT])
    return outputs(meta, 5, mine, move(mine, perm=SWAP), out)


def solution(mesh):
    in_specs = (
        P(None, "col", None, None),
        P(None, "col", None, None),
        P("row", "col", None, None, None),
        P("row", "col", None),
    )
    out_specs = P(None, "col", None, None)
    return jax.shard_map(shards, mesh=mesh, in_specs=in_specs, out_specs=out_specs, check_vma=False)
```

```python
import functools

import jax
import jax.numpy as jnp
from jax import lax
from jax.experimental import pallas as pl
from jax.experimental.pallas import tpu as pltpu
from jax.sharding import PartitionSpec as P

LEVELS = 8
PAIRS = 28
BS = 256
NRHS = 512
PIECE = 64
PART = 2 * PIECE
AXES = ("row", "col")
CHUNKS = ((0, 1), (1, 3), (3, 10), (10, 21), (21, 28))
PERMUTED = 2
SHARED = ((0,), (1,), (2,), (3,), (), (4,))
NT = (((1,), (1,)), ((), ()))
BF = jnp.bfloat16
F32 = jnp.float32
TASK = 2 * PAIRS
AT_Y, AT_H, AT_Z, AT_X = (4 * TASK + n for n in range(4))
TEAMS = [[4 * z + x, 4 * z + 4 + x] for z in (0, 2, 4, 6) for x in range(4)]

def moves(to):
    pairs = []
    for y in range(4):
        for h in range(2):
            for z in range(8):
                for x in range(4):
                    ty, th, tz, tx = to(y, h, z, x)
                    pairs.append(((y * 2 + h) * 32 + z * 4 + x, (ty * 2 + th) * 32 + tz * 4 + tx))
    return pairs


def exchange(y, h, z, x):
    return 2 * (z % 2) + y % 2, h, 2 * (z // 2) + y // 2, x


def level_z(s):
    return lambda y, h, z, x: (y, h, (z + 2 * s) % 8, x)


def cross(t):
    return lambda y, h, z, x: (y // 2 * 2 + x // 2, h, z, (y % 2 * 2 + x % 2) ^ t)


SWAP = moves(lambda y, h, z, x: (y, 1 - h, z, x))
NEIGHBOUR = moves(lambda y, h, z, x: (y, h, z ^ 1, x))
EXCHANGE = moves(exchange)
LEVEL_Z = [moves(level_z(s)) for s in range(4)]
FIRST_Z = [moves(lambda *at, s=s: level_z(s)(*exchange(*at))) for s in range(4)]
CROSS = [moves(cross(t)) for t in range(4)]
INVERSES = [
    ((y * 2 + h) * 32 + z * 4 + x, (y * 2 + h) * 32 + (z ^ 1) * 4 + x)
    for y in range(4)
    for h in range(2)
    for z in range(8)
    for x in range(4)
    if y // 2 == z % 2
]
INVERSE_CHUNKS = ((1, 2), (2, 4), (4, 8))
ALONG_Y = [moves(lambda y, h, z, x, s=s: ((y + s) % 4, h, z, x)) for s in range(4)]
COLLECT = [
    moves(lambda y, h, z, x, s=s: ((2 * (z % 2) + y % 2 + s) % 4, h, 2 * (z // 2) + y // 2, x)) for s in range(4)
]


def dot_nt(a, b):
    return lax.dot_general(a, b, NT, preferred_element_type=F32)


def pair_of(level, earlier):
    return level * (level - 1) // 2 + earlier


def chunk_of(pair):
    return next((n, pair - a) for n, (a, b) in enumerate(CHUNKS) if a <= pair < b)


def factor_spec(pair, side):
    chunk, at = chunk_of(pair)
    if side % 2 == 0:
        return pl.BlockSpec((1, 1, 2, BS, BS), lambda i, meta: (pair, 0, 0, 0, 0))
    if chunk < PERMUTED:
        return pl.BlockSpec((1, 1, 2, BS, BS), lambda i, meta: (at, 0, 0, 0, 0))
    return pl.BlockSpec((1, 1, 1, 2, BS, BS), lambda i, meta: (1 - meta[AT_Z], at, 0, 0, 0, 0))


def factor_of(pair, side, factors):
    if side % 2 == 0:
        return in_hbm(factors[side])
    chunk = chunk_of(pair)[0]
    return factors[side][chunk] if chunk < PERMUTED else in_hbm(factors[side][chunk])


def in_hbm(value):
    return pltpu.with_memory_space_constraint(value, pltpu.HBM)


def whole(shape):
    return pl.BlockSpec(shape, lambda i, meta: (0,) * len(shape))


def call(body, name, grid, specs, out_specs, out_shape, scratch, mib, flops, size, alias=None):
    return pl.pallas_call(
        body,
        name=name,
        grid_spec=pltpu.PrefetchScalarGridSpec(
            num_scalar_prefetch=1,
            grid=grid,
            in_specs=specs,
            out_specs=out_specs,
            scratch_shapes=scratch,
        ),
        out_shape=out_shape,
        compiler_params=pltpu.CompilerParams(vmem_limit_bytes=mib << 20),
        cost_estimate=pl.CostEstimate(flops=flops, bytes_accessed=size, transcendentals=0),
        input_output_aliases=alias or {},
    )


def task_term(meta, pair, side, sources, blocks):
    at = side * TASK + 2 * pair
    lead = (0,) * (len(blocks.shape) - 3)
    return dot_nt(sources[meta[at]], blocks[(*lead, 0)]) + dot_nt(sources[meta[at + 1]], blocks[(*lead, 1)])


def earlier_terms(level, meta, sources, factors):
    count = level - 1
    specs, operands = [], []
    for m in range(count):
        pair = pair_of(level, m)
        specs.append(whole((8, PART, BS)))
        operands.append(in_hbm(sources[m]))
        for side in range(4):
            specs.append(factor_spec(pair, side))
            operands.append(factor_of(pair, side, factors))

    def body(meta, *refs):
        ins, out = refs[:-1], refs[-1]
        for row in range(2):
            total = None
            for m in range(count):
                for side in (row, row + 2):
                    term = task_term(meta, pair_of(level, m), side, ins[5 * m], ins[5 * m + 1 + side])
                    total = term if total is None else total + term
            out[row] = total

    return call(
        body, f"earlier_{level}", (1,), specs, whole((2, PART, BS)),
        jax.ShapeDtypeStruct((2, PART, BS), F32), [], 6 + 4 * count,
        count * 8 * BS**3, count * (3 << 19),
    )(meta, *operands)


def last_term(level, meta, arrived, before, factors):
    pair = pair_of(level, level - 1)
    specs = [whole((4, PIECE, BS))] * 4 + [factor_spec(pair, side) for side in range(4)]
    operands = [*arrived] + [factor_of(pair, side, factors) for side in range(4)]
    if before is not None:
        specs.append(whole((2, PART, BS)))
        operands.append(before)

    def body(meta, *refs):
        ins, outs, total = refs[: len(operands)], refs[len(operands) : -1], refs[-1]
        sources = outs[0]
        for t in range(4):
            at = t // 2 * PIECE
            sources[t % 2 * 4 : t % 2 * 4 + 4, at : at + PIECE, :] = ins[t][...]
        for row in range(2):
            value = None if before is None else ins[8][row]
            for side in (row, row + 2):
                term = task_term(meta, pair, side, sources, ins[4 + side])
                value = term if value is None else value + term
            total[row] = value
        y, z, x = meta[AT_Y], meta[AT_Z], meta[AT_X]
        for s in range(4):
            to = (y + s) % 4
            rows = pl.multiple_of((to + x // 2) % 2 * PIECE, PIECE)
            outs[1 + s][...] = total[(to // 2 + z) % 2, pl.ds(rows, PIECE), :].astype(BF)

    out = call(
        body, f"last_{level}", (1,), specs, [whole((8, PART, BS))] + [whole((PIECE, BS))] * 4,
        [pltpu.HBM((8, PART, BS), BF)] + [jax.ShapeDtypeStruct((PIECE, BS), BF)] * 4,
        [pltpu.VMEM((2, PART, BS), F32)], 10, 8 * BS**3, 3 << 20,
    )(meta, *operands)
    return out[0], out[1:]


def columns_of(meta, right):
    first = meta[AT_H] * BS + meta[AT_Y] * PIECE
    rows = lax.broadcasted_iota(jnp.int32, (PIECE, NRHS), 0)
    columns = lax.broadcasted_iota(jnp.int32, (PIECE, NRHS), 1)
    return dot_nt((columns == rows + first).astype(F32).astype(BF), right).astype(BF)


def solve_first(meta, right_side, inverses):
    def body(meta, right, inverse, out):
        out[...] = dot_nt(columns_of(meta, right[0, 0]), inverse[0, 0]).astype(BF)

    return call(
        body, "solve_0", (1,), [whole((1, 1, BS, NRHS)), whole((1, 1, BS, BS))], whole((PIECE, BS)),
        jax.ShapeDtypeStruct((PIECE, BS), BF), [], 16, 3 * PIECE * BS * NRHS, 1 << 19,
    )(meta, right_side, inverses)


def right_pieces(meta, right_side):
    def body(meta, right, out):
        out[0] = columns_of(meta, right[0, 0])

    return call(
        body, "right_pieces", (LEVELS,), [pl.BlockSpec((1, 1, BS, NRHS), lambda i, meta: (i, 0, 0, 0))],
        pl.BlockSpec((1, PIECE, BS), lambda i, meta: (i, 0, 0)),
        jax.ShapeDtypeStruct((LEVELS, PIECE, BS), BF), [], 16, LEVELS * 2 * PIECE * BS * NRHS, 5 << 19,
    )(meta, right_side)


def solve(level, meta, pieces, rights, inverses, passed):
    n, first = next((n, a) for n, (a, b) in enumerate(INVERSE_CHUNKS) if a <= level < b)

    def body(meta, *refs):
        parts, (right, own, near, out) = refs[:-4], refs[-4:]
        summed = parts[0][...].astype(F32)
        for part in parts[1:]:
            summed = summed + part[...].astype(F32)
        scaled = (right[0].astype(F32) - summed).astype(BF)
        here = meta[AT_Y] // 2 == meta[AT_Z]

        @pl.when(here)
        def _():
            out[...] = dot_nt(scaled, own[0, 0]).astype(BF)

        @pl.when(jnp.logical_not(here))
        def _():
            out[...] = dot_nt(scaled, near[0, 0]).astype(BF)

    specs = [whole((PIECE, BS))] * len(pieces) + [
        pl.BlockSpec((1, PIECE, BS), lambda i, meta: (max(level - 2, 0), 0, 0)),
        pl.BlockSpec((1, 1, BS, BS), lambda i, meta: (level, 0, 0, 0)),
        pl.BlockSpec((1, 1, BS, BS), lambda i, meta: (level - first, 0, 0, 0)),
    ]
    return call(
        body, f"solve_{level}", (1,), specs, whole((PIECE, BS)),
        jax.ShapeDtypeStruct((PIECE, BS), BF), [], 6, 2 * PIECE * BS * BS, 1 << 18,
    )(meta, *pieces, rights[min(level - 1, 1)], inverses, passed[n])


def turned(stacked):
    rows = lax.broadcasted_iota(jnp.int32, (BS, BS), 0)
    columns = lax.broadcasted_iota(jnp.int32, (BS, BS), 1)
    return dot_nt((rows == columns).astype(F32).astype(BF), stacked).astype(BF)


def outputs(meta, start, mine, others, out=None):
    count = mine.shape[1]

    def body(meta, mine, others, *refs):
        out, stacked = refs[-2:]
        y, h = meta[AT_Y], meta[AT_H]
        for side, half in ((mine, h), (others, 1 - h)):
            for s in range(4):
                at = pl.multiple_of(half * BS + ((y - s + 4) % 4) * PIECE, PIECE)
                stacked[pl.ds(at, PIECE), :] = side[s, 0]
        out[0, 0] = turned(stacked[...])

    return call(
        body, f"outputs_{start}", (count,),
        [pl.BlockSpec((4, 1, PIECE, BS), lambda i, meta: (0, i, 0, 0))] * 2
        + [pl.BlockSpec(memory_space=pl.ANY)] * (out is not None),
        pl.BlockSpec((1, 1, BS, NRHS), lambda i, meta: (start + i, 0, 0, 0)),
        jax.ShapeDtypeStruct((LEVELS, 1, BS, NRHS), BF),
        [pltpu.VMEM((NRHS, BS), BF)], 6, count * 2 * BS * BS * NRHS, count << 19,
        alias=None if out is None else {3: 0},
    )(meta, mine, others, *(() if out is None else (out,)))


def joined(pieces):
    return jnp.concatenate(pieces).reshape(len(pieces), *pieces[0].shape)


def after(value, event):
    return lax.optimization_barrier((value, event))[0]


def shards(right_side, inverses, factor_blocks, pattern):
    row, col = lax.axis_index("row"), lax.axis_index("col")
    y, h, z, x = row // 2, row % 2, col // 4, col % 4
    move = functools.partial(lax.ppermute, axis_name=AXES)

    places = jnp.stack([y, h, z % 2, x]).astype(jnp.int32)
    start = jnp.concatenate([jnp.zeros((4 * TASK,), jnp.int32), places])
    solved = solve_first(start, right_side, inverses)

    picked = pattern.reshape(1, TASK)
    picked = jnp.concatenate([picked, move(picked, perm=SWAP)])
    picked = jnp.stack([picked, move(picked, perm=NEIGHBOUR)], axis=1)
    group = (jnp.stack([h, 1 - h]) + x) % 2
    place = 4 * group[:, None, None] + (z // 2 - picked + 8) % 4
    meta = jnp.concatenate([place.reshape(4 * TASK).astype(jnp.int32), places])

    core = move(factor_blocks, perm=SWAP)
    near, far = [None] * len(CHUNKS), [None] * len(CHUNKS)
    factors = [factor_blocks, near, core, far]

    def both(value):
        return lax.all_gather(value, "col", axis_index_groups=TEAMS)

    def fetch(n, event):
        part = after(factor_blocks[CHUNKS[n][0] : CHUNKS[n][1]], event)
        near[n] = move(part, perm=NEIGHBOUR) if n < PERMUTED else both(part)

    def share(n, event):
        far[n] = move(after(near[n], event), perm=SWAP)

    fetch(0, start)
    fetch(2, start)
    first = move(inverses[1:2], perm=INVERSES)
    columns = right_pieces(start, right_side)
    right = move(columns[1:2], perm=EXCHANGE)
    solved, meta, near[0], first, right = lax.optimization_barrier((solved, meta, near[0], first, right))
    passed, rights = [first], [right]

    sources = []
    for level in range(1, LEVELS):
        if level == 1:
            held = [move(solved, perm=way) for way in FIRST_Z]
            solutions = held[:1]
            block = joined(held)
            rights.append(move(after(columns[2:], block), perm=EXCHANGE))
        else:
            block = joined([solved] + [move(solved, perm=way) for way in LEVEL_Z[1:]])
        arrived = [move(block, perm=way) for way in CROSS]
        if level < PERMUTED:
            fetch(level, block)
        if level <= len(SHARED):
            for n in SHARED[level - 1]:
                share(n, block)
        if level < 3:
            fetch(level + 2, block)
        if level < len(INVERSE_CHUNKS):
            a, b = INVERSE_CHUNKS[level]
            passed.append(move(after(inverses[a:b], block), perm=INVERSES))
        if level == 6:
            early = [move(after(joined(solutions[:5]), block), perm=way) for way in COLLECT]
        if level == 7:
            mine = joined(early)
            out = outputs(meta, 0, mine, move(after(mine, block), perm=SWAP))
        before = None
        if level > 1:
            before = earlier_terms(level, meta, sources, factors)
        stacked, parts = last_term(level, meta, arrived, before, factors)
        sources.append(stacked)
        pieces = [parts[0]] + [move(parts[s], perm=ALONG_Y[s]) for s in (1, 2, 3)]
        if level == LEVELS - 1:
            pieces, out = lax.optimization_barrier((pieces, out))
        solved = solve(level, meta, pieces, rights, inverses, passed)
        solutions.append(solved)

    tail = joined(solutions[5:])
    mine = joined([move(tail, perm=way) for way in COLLECT])
    return outputs(meta, 5, mine, move(mine, perm=SWAP), out)


def solution(mesh):
    in_specs = (
        P(None, "col", None, None),
        P(None, "col", None, None),
        P("row", "col", None, None, None),
        P("row", "col", None),
    )
    out_specs = P(None, "col", None, None)
    return jax.shard_map(shards, mesh=mesh, in_specs=in_specs, out_specs=out_specs, check_vma=False)
```
